32 devices in a mesh: dp: 8 (over z, x), tensor: 4 (over y, core).
Axes of the slice: x: 2, y: 2, z: 4, core: 2. Of those that a mesh axis runs over, the one named last changes fastest.
Arguments:
- tokens: bfloat16 [16384, 768], P('dp'), may hold values from -6 to 6
- segments: int32 [16, 1024], P('dp'), may hold values from 0 to 7, never falling along the last dimension, each value on 1 to 512 neighbouring positions
- w_query: bfloat16 [768, 768], P(None, 'tensor'), may hold values from -0.3125 to 0.3125
- b_query: bfloat16 [768], P('tensor'), may hold values from -3 to 3
- w_key: bfloat16 [768, 768], P(None, 'tensor'), may hold values from -0.3125 to 0.3125
- w_value: bfloat16 [768, 768], P(None, 'tensor'), may hold values from -0.21875 to 0.21875
- b_value: bfloat16 [768], P('tensor'), may hold values from -3 to 3
- w_out: bfloat16 [768, 768], P('tensor'), may hold values from -0.875 to 0.875
- b_out: float32 [768], replicated, may hold values from -2 to 2
- gain_one: float32 [768], replicated, may hold values from 0.5 to 1.5
- shift_one: float32 [768], replicated, may hold values from -2 to 2
- w_up: bfloat16 [768, 3072], P(None, 'tensor'), may hold values from -0.21875 to 0.21875
- b_up: float32 [3072], P('tensor'), may hold values from -3 to 3
- w_down: bfloat16 [3072, 768], P('tensor'), may hold values from -0.21875 to 0.21875
- b_down: float32 [768], replicated, may hold values from -2 to 2
- gain_two: float32 [768], replicated, may hold values from 0.5 to 1.5
- shift_two: float32 [768], replicated, may hold values from -2 to 2
- head_gate: float32 [12], P('tensor'), may hold values from 0.2 to 1
- unit_gate: float32 [3072], P('tensor'), may hold values from 0.2 to 1
- hidden_gate: float32 [768], replicated, may hold values from 0.4 to 1
- branch_gate: float32 [2], replicated, may hold values from 0.5 to 1
- cotangent: bfloat16 [16384, 768], P('dp'), may hold values from -6 to 6
Outputs:
- out: bfloat16 [16384, 768], P(('dp', 'tensor'))
- tokens_grad: float32 [16384, 768], P(('dp', 'tensor'))
- w_query_grad: float32 [768, 768], P('dp', 'tensor')
- b_query_grad: float32 [768], P('tensor')
- w_key_grad: float32 [768, 768], P('dp', 'tensor')
- w_value_grad: float32 [768, 768], P('dp', 'tensor')
- b_value_grad: float32 [768], P('tensor')
- w_out_grad: float32 [768, 768], P('tensor', 'dp')
- b_out_grad: float32 [768], replicated
- gain_one_grad: float32 [768], replicated
- shift_one_grad: float32 [768], replicated
- w_up_grad: float32 [768, 3072], P('dp', 'tensor')
- b_up_grad: float32 [3072], P('tensor')
- w_down_grad: float32 [3072, 768], P('tensor', 'dp')
- b_down_grad: float32 [768], replicated
- gain_two_grad: float32 [768], replicated
- shift_two_grad: float32 [768], replicated
- head_gate_grad: float32 [12], P('tensor')
- unit_gate_grad: float32 [3072], P('tensor')
- hidden_gate_grad: float32 [768], replicated
- branch_gate_grad: float32 [2], replicated
The draws below stay inside these ranges and needn't reach their ends.
Inputs may be any that keep to these rules, and one draw needn't show every extreme that they name: `segments`: within each sequence the numbers never fall; each of the 8 documents has 1 to 512 tokens, one exactly 512.
All inputs are finite; a program needn't handle non-finite values.
Results may differ from the reference program's by a relative error of at most 0.013.
The reference program's roundings to bfloat16 on the way count: a program that leaves them out, or rounds other values in their place, can miss the bound.
Values may be sent and summed in bfloat16 or wider, within the bound.
No kernel may reach another device: no remote copies, remote signals or barrier semaphores. Data moves between devices by JAX's collectives and lax.ppermute only.
A program may use at most 128 MiB of HBM per device.

```python
import math
import jax
import jax.numpy as jnp
import numpy as np
from jax import lax

D = 768
HEADS = 12
HEAD_DIM = 64
FF = 3072
LEN = 1024
DOCS = 8
DOC_MOST = 512
SEQS = 16
TOKENS = 16384


def spiked(values, key, source, target, blocks, factor):
    def block_of(axis_at):
        return (jnp.arange(values.shape[axis_at]) // (values.shape[axis_at] // blocks)).reshape((-1,) + (1,) * (values.ndim - 1 - axis_at))

    near = jax.random.permutation(key, blocks)[block_of(target)]
    far = (block_of(target) + blocks // 2) % blocks
    return jnp.where((block_of(source) == near) | (block_of(source) == far), factor * values, values)


def block_scale(stream_key, dims, split, low, top_value):
    level, own = 1.0, jax.random.fold_in(stream_key, 6)
    for position, shards_of in split:
        draws = jnp.exp(jax.random.uniform(jax.random.fold_in(own, position), (shards_of,), jnp.float32, low / len(split), top_value / len(split)))
        level = level * jnp.repeat(draws, dims[position] // shards_of).reshape([-1 if axis == position else 1 for axis in range(len(dims))])
    return level


def length_profile(count, total, most, slope):
    weights = [(1 << 20) // math.isqrt(grade ** slope) + 1 for grade in range(2, count + 1)]
    spare, given = total - most - (count - 1), [1] * (count - 1)
    while spare > 0:
        movable = [i for i in range(count - 1) if given[i] < most]
        pool, left = sum([weights[i] for i in movable]), spare
        for i in movable:
            more = min(most - given[i], max(1, left * weights[i] // pool), spare)
            given[i] = given[i] + more
            spare = spare - more
    return np.array([most] + given)


def ragged(stream_key, count, total, most, skew):
    if count == 2:
        one = jax.random.randint(stream_key, (), max(1, total - most), min(most, total - 1) + 1)
        return jnp.stack([one, total - one])
    lengths = jnp.asarray(length_profile(count, total, most, skew), jnp.int32)
    pairs = (count - 1) // 2
    giver, receiver = lengths[1:1 + 2 * pairs:2], lengths[2:2 + 2 * pairs:2]
    slack = jnp.minimum(giver - 1, most - receiver)
    moved = jax.random.randint(jax.random.fold_in(stream_key, 1), (pairs,), 0, 1 << 20) % (slack + 1)
    lengths = lengths.at[1:1 + 2 * pairs:2].set(giver - moved).at[2:2 + 2 * pairs:2].set(receiver + moved)
    return lengths[jax.random.permutation(jax.random.fold_in(stream_key, 2), count)]


def normal_values(rng, dims, scale, limit, pieces=(), held_as=jnp.bfloat16):
    array = scale * jax.random.normal(rng, dims, jnp.float32)
    if pieces:
        array = array * block_scale(rng, dims, pieces, -0.22, 0.18)
    return jnp.clip(array, -limit, limit).astype(held_as)


def heavy_noise(rng, shape, width, most, split, heavy, dtype=jnp.bfloat16):
    entries = width * jax.random.normal(rng, shape, jnp.float32)
    if split:
        entries = entries * block_scale(rng, shape, split, -0.22, 0.18)
    return jnp.clip(spiked(entries, jax.random.fold_in(rng, 3), *heavy), -most, most).astype(dtype)


def setup_inputs(seed: int = 0) -> dict:
    keys = jax.random.split(jax.random.key(seed), 23)
    return {
        "tokens": heavy_noise(keys[0], (TOKENS, D), 1.0, 6.0, ((0, 8),), (0, 1, 8, 2.0)),
        "segments": jax.vmap(lambda own: jnp.searchsorted(jnp.cumsum(ragged(own, DOCS, LEN, DOC_MOST, 2)), jnp.arange(LEN), side="right"))(jax.random.split(keys[1], SEQS)).reshape((SEQS, LEN)).astype(jnp.int32),
        "w_query": normal_values(keys[2], (D, D), (D // 2) ** -0.5, 0.3125, ((1, 4),)),
        "b_query": normal_values(keys[3], (D,), 0.5, 3.0, ((0, 4),)),
        "w_key": normal_values(keys[4], (D, D), (D // 2) ** -0.5, 0.3125, ((1, 4),)),
        "w_value": normal_values(keys[5], (D, D), D ** -0.5, 0.21875, ((1, 4),)),
        "b_value": normal_values(keys[6], (D,), 0.5, 3.0, ((0, 4),)),
        "w_out": normal_values(keys[7], (D, D), (D // 16) ** -0.5, 0.875, ((0, 4),)),
        "b_out": normal_values(keys[8], (D,), 0.3, 2.0, (), jnp.float32),
        "gain_one": jnp.clip(1.0 + 0.1 * jax.random.normal(keys[9], (D,), jnp.float32), 0.5, 1.5),
        "shift_one": normal_values(keys[10], (D,), 0.3, 2.0, (), jnp.float32),
        "w_up": normal_values(keys[11], (D, FF), D ** -0.5, 0.21875, ((1, 4),)),
        "b_up": normal_values(keys[12], (FF,), 0.5, 3.0, ((0, 4),), jnp.float32),
        "w_down": normal_values(keys[13], (FF, D), (FF // 4) ** -0.5, 0.21875, ((0, 4),)),
        "b_down": normal_values(keys[14], (D,), 0.3, 2.0, (), jnp.float32),
        "gain_two": jnp.clip(1.0 + 0.1 * jax.random.normal(keys[15], (D,), jnp.float32), 0.5, 1.5),
        "shift_two": normal_values(keys[16], (D,), 0.3, 2.0, (), jnp.float32),
        "head_gate": jnp.clip(0.2 + 0.8 * jax.random.uniform(keys[17], (HEADS,), jnp.float32) ** block_scale(keys[17], (HEADS,), ((0, 4),), -0.2, 0.2), 0.2, 1.0),
        "unit_gate": jnp.clip(0.2 + 0.8 * jax.random.uniform(keys[18], (FF,), jnp.float32) ** block_scale(keys[18], (FF,), ((0, 4),), -0.2, 0.2), 0.2, 1.0),
        "hidden_gate": jnp.clip(jax.random.uniform(keys[19], (D,), jnp.float32, 0.4, 1.0), 0.4, 1.0),
        "branch_gate": jnp.clip(jax.random.uniform(keys[20], (2,), jnp.float32, 0.5, 1.0), 0.5, 1.0),
        "cotangent": heavy_noise(keys[21], (TOKENS, D), 1.0, 6.0, ((0, 8),), (0, 1, 8, 2.0)),
    }


@jax.custom_vjp
def low(v):
    return lax.optimization_barrier(v.astype(jnp.bfloat16)).astype(jnp.float32)

@jax.custom_vjp
def low_back(v):
    return v

def low_keep(v):
    return (low(v), None)

def low_pass(kept, grad):
    return (grad,)

def back_keep(v):
    return (v, None)

def back_low(kept, grad):
    return (low(grad),)
low.defvjp(low_keep, low_pass)
low_back.defvjp(back_keep, back_low)

def matmul(operand, matrix):
    return jnp.dot(operand, matrix, precision=lax.Precision.HIGHEST)

def normalize(row_data):
    centre = row_data - lax.optimization_barrier(jnp.mean(row_data, axis=-1, keepdims=True))
    return centre * lax.rsqrt(lax.optimization_barrier(jnp.mean(centre * centre, axis=-1, keepdims=True)) + 1e-12)

def layer(token_rows, w_query, b_query, w_key, w_value, b_value, w_out, b_out, gain_one, shift_one, w_up, b_up, w_down, b_down, gain_two, shift_two, head_gate, unit_gate, hidden_gate, branch_gate, doc_ids):
    queries = low(low_back(matmul(token_rows, w_query) + b_query)).reshape(LEN, HEADS, HEAD_DIM)
    key_rows = low(low_back(matmul(token_rows, w_key))).reshape(LEN, HEADS, HEAD_DIM)
    value_rows = low(low_back(matmul(token_rows, w_value) + b_value)).reshape(LEN, HEADS, HEAD_DIM)
    scores = low_back(jnp.einsum('qhd,khd->hqk', queries, key_rows, precision=lax.Precision.HIGHEST) * 0.125)
    same_doc = doc_ids[:, None] == doc_ids[None, :]
    scores = jnp.where(same_doc[None], scores, -1e+30)
    attention = jax.nn.softmax(scores, axis=-1)
    context = jnp.einsum('hqk,khd->qhd', low(attention), value_rows, precision=lax.Precision.HIGHEST).reshape(LEN, D)
    gated_context = low(low_back(context) * jnp.repeat(head_gate, HEAD_DIM)[None, :])
    attn_sum = low_back(matmul(gated_context, w_out))
    branch = (attn_sum + b_out) * branch_gate[0] * hidden_gate
    normed = (normalize(token_rows + branch) * gain_one + shift_one) * hidden_gate
    up_in = low_back(matmul(low(normed), w_up) + b_up)
    unit_out = low(jax.nn.gelu(up_in, approximate=False) * unit_gate)
    down_sum = low_back(matmul(unit_out, w_down))
    branch_two = (down_sum + b_down) * branch_gate[1] * hidden_gate
    return (normalize(normed + branch_two) * gain_two + shift_two) * hidden_gate

def reference(tokens, segments, w_query, b_query, w_key, w_value, b_value, w_out, b_out, gain_one, shift_one, w_up, b_up, w_down, b_down, gain_two, shift_two, head_gate, unit_gate, hidden_gate, branch_gate, cotangent):
    params = tuple((argument.astype(jnp.float32) for argument in (w_query, b_query, w_key, w_value, b_value, w_out, b_out, gain_one, shift_one, w_up, b_up, w_down, b_down, gain_two, shift_two, head_gate, unit_gate, hidden_gate, branch_gate)))
    token_rows = tokens.astype(jnp.float32).reshape(SEQS, LEN, D)
    grad_rows = cotangent.astype(jnp.float32).reshape(SEQS, LEN, D)

    def one_sequence(totals, inputs):
        seq_rows, seq_grad, doc_ids = inputs

        def forward(seq_input, *weights):
            return layer(seq_input, *weights, doc_ids)
        result, pullback = jax.vjp(forward, seq_rows, *params)
        gradients = pullback(seq_grad)
        totals = tuple((running + update for running, update in zip(totals, gradients[1:])))
        return (totals, (result, gradients[0]))
    start_sums = tuple((jnp.zeros_like(argument) for argument in params))
    totals, (outputs, input_grads) = lax.scan(one_sequence, start_sums, (token_rows, grad_rows, segments))
    return (outputs.reshape(TOKENS, D).astype(jnp.bfloat16), input_grads.reshape(TOKENS, D), totals[0], totals[1], totals[2], totals[3], totals[4], totals[5], totals[6], totals[7], totals[8], totals[9], totals[10], totals[11], totals[12], totals[13], totals[14], totals[15], totals[16], totals[17], totals[18])
```

```python
import jax
import jax.numpy as jnp
from jax import lax
from jax.sharding import PartitionSpec as P

HEAD_DIM = 64
LEN = 1024
WIDTH = 768
F32 = jnp.float32
BF16 = jnp.bfloat16


def normalize(row_data):
    centre = row_data - jnp.mean(row_data, axis=-1, keepdims=True)
    return centre * lax.rsqrt(jnp.mean(centre * centre, axis=-1, keepdims=True) + 1e-12)


def attention_rows(attn_sum, token_rows, b_out, gain_one, shift_one, hidden_gate, first_gate):
    branch = (attn_sum + b_out) * first_gate * hidden_gate
    return (normalize(token_rows + branch) * gain_one + shift_one) * hidden_gate


def output_rows(down_sum, normed, b_down, gain_two, shift_two, hidden_gate, second_gate):
    branch = (down_sum + b_down) * second_gate * hidden_gate
    return (normalize(normed + branch) * gain_two + shift_two) * hidden_gate


def exact_gelu(inputs):
    return jax.nn.gelu(inputs, approximate=False)


def swap(array, axis, bit):
    size = lax.axis_size(axis)
    return lax.ppermute(array, axis, [(i, i ^ bit) for i in range(size)])


def dot(left, right, left_dim, right_dim):
    return lax.dot_general(
        left, right, (((left_dim,), (right_dim,)), ((), ())), preferred_element_type=F32
    )


def attend(queries, keys, values, same_doc):
    heads = queries.shape[1] // HEAD_DIM
    split = lambda a: a.reshape(LEN, heads, HEAD_DIM)
    scores = jnp.einsum("qhd,khd->hqk", split(queries), split(keys), preferred_element_type=F32) * 0.125
    scores = jnp.where(same_doc[None], scores, -1e30)
    peak = jnp.max(scores, axis=-1, keepdims=True)
    exponent = jnp.exp(scores - peak)
    mass = jnp.sum(exponent, axis=-1, keepdims=True)
    attention = (exponent / mass).astype(BF16)
    context = jnp.einsum("hqk,khd->qhd", attention, split(values), preferred_element_type=F32)
    return context.reshape(LEN, heads * HEAD_DIM), peak + jnp.log(mass)


def attend_back(queries, keys, values, same_doc, log_mass, context_grad):
    heads = queries.shape[1] // HEAD_DIM
    split = lambda a: a.reshape(LEN, heads, HEAD_DIM)
    join = lambda a: a.reshape(LEN, heads * HEAD_DIM).astype(BF16)
    q, k, v, g = split(queries), split(keys), split(values), split(context_grad)
    scores = jnp.einsum("qhd,khd->hqk", q, k, preferred_element_type=F32) * 0.125
    scores = jnp.where(same_doc[None], scores, -1e30)
    attention = jnp.exp(scores - log_mass)
    prob_grad = jnp.einsum("qhd,khd->hqk", g, v, preferred_element_type=F32)
    centred = prob_grad - jnp.sum(attention * prob_grad, axis=-1, keepdims=True)
    score_grad = (attention * centred).astype(BF16)
    query_grad = jnp.einsum("hqk,khd->qhd", score_grad, k, preferred_element_type=F32) * 0.125
    key_grad = jnp.einsum("hqk,qhd->khd", score_grad, q, preferred_element_type=F32) * 0.125
    value_grad = jnp.einsum("hqk,qhd->khd", attention.astype(BF16), g, preferred_element_type=F32)
    return join(query_grad), join(key_grad), join(value_grad)


def fold(grad, axis, bit, rank_bit):
    kept = jnp.where(rank_bit == 0, grad[0], grad[1])
    sent = jnp.where(rank_bit == 0, grad[1], grad[0])
    received = swap(sent.astype(BF16), axis, bit)
    return kept.astype(F32) + received.astype(F32)


def fold_rows(grad, dp_rank, dp_size, first=0):
    bit = 1 << first
    while bit < dp_size:
        blocks, rows, cols = grad.shape
        pairs = grad.reshape(blocks // 2, 2, rows, cols).swapaxes(0, 1)
        grad = fold(pairs, "dp", bit, (dp_rank // bit) % 2)
        bit *= 2
    return grad[0]


def local(
    tokens, segments, w_query, b_query, w_key, w_value, b_value, w_out, b_out, gain_one, shift_one,
    w_up, b_up, w_down, b_down, gain_two, shift_two, head_gate, unit_gate, hidden_gate, branch_gate, cotangent,
):
    rank = lax.axis_index("tensor")
    core, seq = rank % 2, rank // 2
    dp_rank, dp_size = lax.axis_index("dp"), lax.axis_size("dp")
    half = LEN // 2
    attn_own = jnp.concatenate([w_query.T, w_key.T, w_value.T, w_out], axis=0)
    pad = jnp.zeros((WIDTH - 387,), F32)
    small_own = jnp.stack(
        [jnp.concatenate([b_query.astype(F32), b_value.astype(F32), head_gate, pad]), b_up, unit_gate]
    )
    attn_far = swap(attn_own, "tensor", 2)
    small_far = swap(small_own, "tensor", 2)
    mlp_own = jnp.stack([w_up, w_down])
    mlp_far = swap(mlp_own, "tensor", 2)
    mlp_core = swap(mlp_own, "tensor", 1)
    mlp_far_core = swap(mlp_far, "tensor", 1)
    small_core = swap(jnp.stack([small_own, small_far]), "tensor", 1)
    seq_tokens = lax.dynamic_slice_in_dim(tokens, seq * LEN, LEN, 0)
    doc_ids = lax.dynamic_slice_in_dim(segments, seq, 1, 0)[0]
    same_doc = doc_ids[:, None] == doc_ids[None, :]
    attn_pieces = []
    attn_part = 0.0
    for weights, small in ((attn_own, small_own), (attn_far, small_far)):
        both = dot(seq_tokens, weights[:576], 1, 1)
        bias_q, bias_v, gates = small[0, :192], small[0, 192:384], small[0, 384:387]
        queries = (both[:, :192] + bias_q).astype(BF16)
        keys = both[:, 192:384].astype(BF16)
        values = (both[:, 384:576] + bias_v).astype(BF16)
        context, log_mass = attend(queries, keys, values, same_doc)
        column_gate = jnp.repeat(gates, HEAD_DIM)
        gated = (context * column_gate[None, :]).astype(BF16)
        attn_part = attn_part + dot(gated, weights[576:], 1, 0)
        attn_pieces.append((weights, queries, keys, values, context, log_mass, column_gate, gated))
    own_half = lambda a, which: lax.dynamic_slice_in_dim(a, which * half, half, 0)
    attn_total = own_half(attn_part, core) + swap(own_half(attn_part, 1 - core), "tensor", 1)
    row_tokens = own_half(seq_tokens, core)
    row_cotangent = lax.dynamic_slice_in_dim(cotangent, rank * half, half, 0).astype(F32)
    normed, attn_back = jax.vjp(
        attention_rows, attn_total, row_tokens.astype(F32), b_out, gain_one, shift_one, hidden_gate, branch_gate[0]
    )
    normed_low = normed.astype(BF16)
    mlp = [mlp_own, mlp_core, mlp_far, mlp_far_core]
    units = [small_own, small_core[0], small_far, small_core[1]]
    down_total = 0.0
    saved = []
    for weights, small in zip(mlp, units):
        up_in = dot(normed_low, weights[0], 1, 0) + small[1]
        unit_act, gelu_back = jax.vjp(exact_gelu, up_in)
        unit_out = (unit_act * small[2][None, :]).astype(BF16)
        down_total = down_total + dot(unit_out, weights[1], 1, 0)
        saved.append((unit_act, gelu_back, unit_out))
    result, output_back = jax.vjp(
        output_rows, down_total, normed, b_down, gain_two, shift_two, hidden_gate, branch_gate[1]
    )
    down_grad, normed_res, b_down_grad, gain_two_grad, shift_two_grad, hidden_two, second_grad = output_back(
        row_cotangent
    )
    down_low = down_grad.astype(BF16)
    normed_total = normed_res
    mlp_grads, vec_grads = [], []
    for weights, small, (unit_act, gelu_back, unit_out) in zip(mlp, units, saved):
        w_down_t = dot(down_low, unit_out, 0, 0)
        unit_grad = dot(down_low, weights[1], 1, 1)
        gate_grad = jnp.sum(unit_grad * unit_act, axis=0)
        up_grad = gelu_back(unit_grad * small[2][None, :])[0].astype(BF16)
        b_up_part = jnp.sum(up_grad.astype(F32), axis=0)
        w_up_part = dot(normed_low, up_grad, 0, 0)
        normed_total = normed_total + dot(up_grad, weights[0], 1, 1)
        mlp_grads.append(jnp.concatenate([w_up_part, w_down_t], axis=1))
        vec_grads.append(jnp.stack([b_up_part, gate_grad]))
    attn_grad, token_res, b_out_grad, gain_one_grad, shift_one_grad, hidden_one, first_grad = attn_back(normed_total)
    attn_low = attn_grad.astype(BF16)
    other_low = swap(attn_low, "tensor", 1)
    attn_rows = jnp.where(
        core == 0, jnp.concatenate([attn_low, other_low]), jnp.concatenate([other_low, attn_low])
    )
    received = swap(jnp.stack([mlp_grads[1], mlp_grads[3]]).astype(BF16), "tensor", 1).astype(F32)
    near, far = mlp_grads[0] + received[0], mlp_grads[2] + received[1]
    mlp_sum = near + swap(far.astype(BF16), "tensor", 2).astype(F32)
    mlp_block = fold_rows(mlp_sum.reshape(dp_size, WIDTH // dp_size, 2 * WIDTH), dp_rank, dp_size)
    token_part = 0.0
    attn_grads, head_vecs = [], []
    for weights, queries, keys, values, context, log_mass, column_gate, gated in attn_pieces:
        w_out_t = dot(attn_rows, gated, 0, 0)
        gated_grad = dot(attn_rows, weights[576:], 1, 1)
        head_grad = jnp.sum((gated_grad * context).reshape(-1, 3, HEAD_DIM), axis=(0, 2))
        context_grad = (gated_grad * column_gate[None, :]).astype(BF16)
        grads = jnp.concatenate(
            attend_back(queries, keys, values, same_doc, log_mass, context_grad), axis=1
        )
        sums = jnp.sum(grads.astype(F32), axis=0)
        head_vecs.append(jnp.concatenate([sums[:192], sums[384:], head_grad, pad]))
        attn_grads.append(jnp.concatenate([dot(seq_tokens, grads, 0, 0), w_out_t], axis=1))
        token_part = token_part + dot(grads, weights[:576], 1, 0)
    token_total = own_half(token_part, core) + swap(own_half(token_part, 1 - core), "tensor", 1)
    tokens_grad = token_total + token_res
    attn_sum = attn_grads[0] + swap(attn_grads[1].astype(BF16), "tensor", 2).astype(F32)
    attn_block = fold_rows(attn_sum.reshape(dp_size, WIDTH // dp_size, WIDTH), dp_rank, dp_size)
    zero = jnp.zeros((WIDTH,), F32)
    branch_row = jnp.concatenate([jnp.stack([first_grad, second_grad]), jnp.zeros((WIDTH - 2,), F32)])
    common = jnp.stack(
        [b_out_grad, gain_one_grad, shift_one_grad, b_down_grad, gain_two_grad, shift_two_grad,
         hidden_one + hidden_two, branch_row]
    )
    quarter_rows = jnp.zeros((4, 3, WIDTH), F32)
    for index, (flip, heads) in enumerate(((0, head_vecs[0]), (1, None), (2, head_vecs[1]), (3, None))):
        block = jnp.concatenate([(zero if heads is None else heads)[None], vec_grads[index]])
        quarter_rows = lax.dynamic_update_slice(quarter_rows, block[None], (rank ^ flip, 0, 0))
    vectors = jnp.concatenate([common, quarter_rows.reshape(12, WIDTH)])
    vectors = vectors + swap(vectors, "tensor", 1)
    vectors = vectors + swap(vectors, "tensor", 2)
    bit = 1
    while bit < dp_size:
        vectors = vectors + swap(vectors, "dp", bit)
        bit *= 2
    mine = lax.dynamic_slice(vectors, (8 + 3 * rank, 0), (3, WIDTH))
    return (
        result.astype(BF16),
        tokens_grad,
        attn_block[:, :192],
        mine[0, :192],
        attn_block[:, 192:384],
        attn_block[:, 384:576],
        mine[0, 192:384],
        attn_block[:, 576:].T,
        vectors[0],
        vectors[1],
        vectors[2],
        mlp_block[:, :WIDTH],
        mine[1],
        mlp_block[:, WIDTH:].T,
        vectors[3],
        vectors[4],
        vectors[5],
        mine[0, 384:387],
        mine[2],
        vectors[6],
        vectors[7, :2],
    )


def solution(mesh):
    row, col = P("dp", None), P(None, "tensor")
    placed = (
        row, row, col, P("tensor"), col, col, P("tensor"), P("tensor", None), P(), P(), P(), col, P("tensor"),
        P("tensor", None), P(), P(), P(), P("tensor"), P("tensor"), P(), P(), row,
    )
    rows, part, turned = P(("dp", "tensor"), None), P("dp", "tensor"), P("tensor", "dp")
    return jax.shard_map(
        local,
        mesh=mesh,
        in_specs=placed,
        out_specs=(
            rows, rows, part, P("tensor"), part, part, P("tensor"), turned, P(), P(), P(), part, P("tensor"),
            turned, P(), P(), P(), P("tensor"), P("tensor"), P(), P(),
        ),
        check_vma=False,
    )
```
